32 devices in a mesh: expert: 8 (over y, x, core), tensor: 4 (over z).
Axes of the slice: x: 2, y: 2, z: 4, core: 2. Of those that a mesh axis runs over, the one named last changes fastest.
Arguments:
- tokens: bfloat16 [1024, 2048], P('expert', 'tensor'), may hold values from -6 to 6
- out_grad: bfloat16 [1024, 2048], P('expert', 'tensor'), may hold values from -6 to 6
- routes: int32 [1024, 6], P('expert'), may hold values from 0 to 15, all different within a row; in each aligned block of 128 rows (0 to 127, 128 to 255, ...) at most 64 rows name the same one
- route_gates: float32 [1024, 6], P('expert'), may hold values from 0.05 to 0.5
- gate_weight: bfloat16 [8, 2816, 2048], P('expert', 'tensor'), may hold values from -0.125 to 0.125
- up_weight: bfloat16 [8, 2816, 2048], P('expert', 'tensor'), may hold values from -0.125 to 0.125
- down_weight: bfloat16 [8, 2816, 2048], P('expert', 'tensor'), may hold values from -0.15625 to 0.15625
Outputs:
- in_grad: bfloat16 [1024, 2048], P('expert', 'tensor')
- grad_gate: bfloat16 [8, 2816, 2048], P('expert', 'tensor')
- grad_up: bfloat16 [8, 2816, 2048], P('expert', 'tensor')
- grad_down: bfloat16 [8, 2816, 2048], P('expert', 'tensor')
The draws below stay inside these ranges and needn't reach their ends.
Inputs may be any that keep to these rules, and one draw needn't show every extreme that they name: `routes`: each row names 6 different experts. In each aligned block of 128 rows (the tokens of one index of expert) no expert is named by more than 64 rows, a bound that some block reaches.
All inputs are finite; a program needn't handle non-finite values.
Results may differ from the reference program's by a relative error of at most 0.015.
Values may be sent and summed in bfloat16 or wider, within the bound.
No kernel may reach another device: no remote copies, remote signals or barrier semaphores. Data moves between devices by JAX's collectives and lax.ppermute only.
A program may use at most 64 MiB of HBM per device.

```python
import math
import jax
import jax.numpy as jnp
import numpy as np
from jax import lax

D = 2048
HID = 1408
TOP = 6
EXP_DEV = 2
TOK_DEV = 128
EXPERTS = 16
CAP = 64
HID_DEV = 704
TOKENS = 1024
N_EXPERT = 8


def block_levels(own_key, shape, pieces, least, top_value):
    def one(axis_at, shards_of):
        draws = jax.random.uniform(jax.random.fold_in(jax.random.fold_in(own_key, 6), axis_at), (shards_of,), jnp.float32, least / len(pieces), top_value / len(pieces))
        return jnp.repeat(jnp.exp(draws), shape[axis_at] // shards_of).reshape((-1,) + (1,) * (len(shape) - axis_at - 1))

    gain = one(*pieces[0])
    for cut in pieces[1:]:
        gain = gain * one(*cut)
    return gain


def assign_block(own_key, own, number, rows, amount, top, bound, slope):
    order = jax.random.permutation(own_key, amount)
    heavy_load, usual = load_shares(amount, rows * top, bound, slope, True), load_shares(amount, rows * top, bound, slope, False)
    places = jnp.arange(amount)

    def named(lengths, rotation):
        used = int((lengths > 0).sum())
        fixed = max(1, used // 4)
        moved = fixed + (places - fixed + rotation * (used - fixed)) % max(1, amount - fixed)
        return jnp.zeros((amount,), jnp.int32).at[order[jnp.where(places < fixed, places, moved)]].set(jnp.asarray(lengths, jnp.int32))

    lengths = jnp.where(number % 4 == 0, named(heavy_load, number // 4), named(usual, number - number // 4 - 1))
    mixed = jax.random.permutation(jax.random.fold_in(own, 3), amount)
    source_of, taker = mixed[0:amount // 2 * 2:2], mixed[1:amount // 2 * 2:2]
    margin = jnp.minimum(lengths[source_of] - 1, bound - lengths[taker]) // 2
    margin = jnp.where((source_of == order[0]) | (taker == order[0]) | (lengths[taker] == 0), 0, jnp.maximum(margin, 0))
    moved = jax.random.randint(jax.random.fold_in(own, 4), (amount // 2,), 0, 1 << 20) % (margin + 1)
    lengths = lengths.at[source_of].add(-moved).at[taker].add(moved)
    items = jnp.searchsorted(jnp.cumsum(lengths), jnp.arange(rows * top), side="right").astype(jnp.int32)
    table = items.reshape(top, rows).T
    table = table[jax.random.permutation(jax.random.fold_in(own, 1), rows)]
    rotation = jax.random.randint(jax.random.fold_in(own, 2), (rows, 1), 0, top)
    return jnp.take_along_axis(table, (jnp.arange(top)[None, :] + rotation) % top, axis=1)


def load_shares(number_of, total, limit, slope, full):
    loads = [(1 << 20) // math.isqrt(rank ** slope) + 1 for rank in range(1, number_of + 1)]
    largest = limit if full else min(limit, max(-(-total // number_of), total * loads[0] // sum(loads)))
    least = 1 if total - largest >= number_of - 1 else 0
    given, spare = [largest] + [least] * (number_of - 1), total - largest - least * (number_of - 1)
    while spare > 0:
        candidates = [i for i in range(1, number_of) if given[i] < largest] or [i for i in range(1, number_of) if given[i] < limit]
        pool, left = sum([loads[i] for i in candidates]), spare
        for i in candidates:
            extra = min(limit - given[i], max(1, left * loads[i] // pool), spare)
            given[i] = given[i] + extra
            spare = spare - extra
    return np.array(given)


def bell_draw(key, shape, deviation, reach, shards=(), kind=jnp.bfloat16):
    loudness = block_levels(key, shape, shards, -0.22, 0.18) if shards else 1.0
    result = jax.random.normal(key, shape, jnp.float32) * deviation * loudness
    return jnp.minimum(jnp.maximum(result, -reach), reach).astype(kind)


def setup_inputs(seed: int = 0) -> dict:
    keys = jax.random.split(jax.random.key(seed), 8)
    tokens = bell_draw(keys[0], (TOKENS, D), 1.0, 6.0, ((0, 8), (1, 4)))
    out_grad = bell_draw(keys[1], (TOKENS, D), 1.0, 6.0, ((0, 8), (1, 4)))
    routes_keys = jax.random.split(jax.random.fold_in(keys[2], 1), TOKENS // TOK_DEV)
    routes_turns = jax.random.permutation(jax.random.fold_in(keys[2], 3), TOKENS // TOK_DEV)
    routes = jax.vmap(lambda own, number: assign_block(jax.random.fold_in(keys[2], 2), own, number, TOK_DEV, EXPERTS, TOP, CAP, 2))(routes_keys, routes_turns).reshape((TOKENS, TOP))
    route_gates = jnp.clip(0.05 + 0.45 * jax.random.uniform(keys[3], (TOKENS, TOP), jnp.float32) ** block_levels(keys[3], (TOKENS, TOP), ((0, 8),), -0.2, 0.2), 0.05, 0.5)
    gate_weight = bell_draw(keys[4], (N_EXPERT, EXP_DEV * HID, D), D ** -0.5, 0.125, ((0, 8), (1, 4)))
    up_weight = bell_draw(keys[5], (N_EXPERT, EXP_DEV * HID, D), D ** -0.5, 0.125, ((0, 8), (1, 4)))
    down_weight = bell_draw(keys[6], (N_EXPERT, EXP_DEV * HID, D), HID ** -0.5, 0.15625, ((0, 8), (1, 4)))
    return {"tokens": tokens, "out_grad": out_grad, "routes": routes, "route_gates": route_gates, "gate_weight": gate_weight, "up_weight": up_weight, "down_weight": down_weight}


def slot_lists(routes, route_gates):
    blocks = routes.reshape(N_EXPERT, TOK_DEV, TOP)
    gate_blocks = route_gates.reshape(N_EXPERT, TOK_DEV, TOP)
    expert_ids = jnp.arange(EXPERTS, dtype=jnp.int32)
    named_hit = blocks[:, :, :, None] == expert_ids[None, None, None, :]
    hit_table = jnp.any(named_hit, axis=2).astype(jnp.int32)
    rank_table = jnp.cumsum(hit_table, axis=1) - hit_table
    gate_table = jnp.sum(jnp.where(named_hit, gate_blocks[:, :, :, None], jnp.float32(0.0)), axis=2)
    source = jnp.arange(N_EXPERT, dtype=jnp.int32)[:, None, None]
    token_ids = source * TOK_DEV + jnp.arange(TOK_DEV, dtype=jnp.int32)[None, :, None]
    token_ids = jnp.broadcast_to(token_ids, (N_EXPERT, TOK_DEV, EXPERTS)).astype(jnp.int32)
    total_slots = EXPERTS * N_EXPERT * CAP
    target = expert_ids[None, None, :] * (N_EXPERT * CAP) + source * CAP + rank_table
    target = jnp.where(hit_table == 1, target, total_slots).astype(jnp.int32)
    slot_tokens = jnp.full((total_slots,), TOKENS, dtype=jnp.int32)
    slot_tokens = slot_tokens.at[target.reshape(-1)].set(token_ids.reshape(-1), mode="drop")
    slot_gates = jnp.zeros((total_slots,), jnp.float32)
    slot_gates = slot_gates.at[target.reshape(-1)].set(gate_table.reshape(-1), mode="drop")
    return slot_tokens.reshape(EXPERTS, N_EXPERT * CAP), slot_gates.reshape(EXPERTS, N_EXPERT * CAP)


def reference(tokens, out_grad, routes, route_gates, gate_weight, up_weight, down_weight):
    slot_tokens, slot_gates = slot_lists(routes, route_gates)
    group_total = HID // HID_DEV
    pad_row = jnp.zeros((1, D), tokens.dtype)
    padded_tokens = jnp.concatenate([tokens, pad_row], axis=0)
    padded_grad = jnp.concatenate([out_grad, pad_row.astype(out_grad.dtype)], axis=0)
    gate_all = gate_weight.reshape(EXPERTS, HID, D)
    up_all = up_weight.reshape(EXPERTS, HID, D)
    down_all = down_weight.reshape(EXPERTS, HID, D)

    def one_expert(operands):
        token_ids, gate_slots, gate_w, up_w, down_w = operands
        rows_x = padded_tokens[token_ids]
        rows_e = (gate_slots[:, None] * padded_grad[token_ids].astype(jnp.float32)).astype(jnp.bfloat16)
        gate_pre = jnp.dot(rows_x, gate_w.T, preferred_element_type=jnp.float32)
        up_pre = jnp.dot(rows_x, up_w.T, preferred_element_type=jnp.float32)
        sigmoid_gate = jax.nn.sigmoid(gate_pre)
        activated = gate_pre * sigmoid_gate
        hidden = (activated * up_pre).astype(jnp.bfloat16)
        dhidden = jnp.dot(rows_e, down_w.T, preferred_element_type=jnp.float32)
        grad_down = jnp.dot(hidden.T, rows_e, preferred_element_type=jnp.float32).astype(jnp.bfloat16)
        grad_pre_gate = (dhidden * up_pre * sigmoid_gate * (1.0 + gate_pre * (1.0 - sigmoid_gate))).astype(jnp.bfloat16)
        grad_pre_up = (dhidden * activated).astype(jnp.bfloat16)
        grad_gate = jnp.dot(grad_pre_gate.T, rows_x, preferred_element_type=jnp.float32).astype(jnp.bfloat16)
        grad_up = jnp.dot(grad_pre_up.T, rows_x, preferred_element_type=jnp.float32).astype(jnp.bfloat16)
        split_gate = grad_pre_gate.astype(jnp.float32).reshape(-1, group_total, HID_DEV)
        split_up = grad_pre_up.astype(jnp.float32).reshape(-1, group_total, HID_DEV)
        weight_gate = gate_w.astype(jnp.float32).reshape(group_total, HID_DEV, D)
        weight_up = up_w.astype(jnp.float32).reshape(group_total, HID_DEV, D)
        shares = jnp.einsum("rsh,shd->rsd", split_gate, weight_gate) + jnp.einsum("rsh,shd->rsd", split_up, weight_up)
        rounded = lax.optimization_barrier(shares.astype(jnp.bfloat16))
        copy_grad = jnp.sum(rounded.astype(jnp.float32), axis=1).astype(jnp.bfloat16)
        return grad_gate, grad_up, grad_down, copy_grad

    grad_gate, grad_up, grad_down, copy_grad = lax.map(
        one_expert, (slot_tokens, slot_gates, gate_all, up_all, down_all))
    copy_grad = lax.optimization_barrier(copy_grad)
    summed = jnp.zeros((TOKENS + 1, D), jnp.float32)
    summed = summed.at[slot_tokens.reshape(-1)].add(copy_grad.reshape(-1, D).astype(jnp.float32))
    in_grad = summed[:TOKENS].astype(jnp.bfloat16)
    shape_out = (N_EXPERT, EXP_DEV * HID, D)
    return in_grad, grad_gate.reshape(shape_out), grad_up.reshape(shape_out), grad_down.reshape(shape_out)
```

```python
import jax
import jax.numpy as jnp
from jax import lax
from jax.sharding import PartitionSpec as P

HID = 1408
EXP_DEV = 2


def slot_tables(routes, route_gates, all_experts, capacity):
    expert_ids = jnp.arange(all_experts, dtype=jnp.int32)
    named_hit = routes[:, :, None] == expert_ids[None, None, :]
    hit_table = jnp.any(named_hit, axis=1).astype(jnp.int32)
    rank_table = jnp.cumsum(hit_table, axis=0) - hit_table
    gate_table = jnp.sum(jnp.where(named_hit, route_gates[:, :, None], jnp.float32(0.0)), axis=1)
    slot_ids = jnp.arange(capacity, dtype=jnp.int32)
    placed = (rank_table.T[:, None, :] == slot_ids[None, :, None]) & (hit_table.T[:, None, :] == 1)
    slot_gate = jnp.sum(jnp.where(placed, gate_table.T[:, None, :], jnp.float32(0.0)), axis=2)
    tok_rows = routes.shape[0]
    dispatch = placed.reshape(all_experts * capacity, tok_rows).astype(jnp.bfloat16)
    return (dispatch, slot_gate.reshape(all_experts * capacity, 1))


def dispatch_shards(tokens, out_grad, routes, route_gates, gate_weight, up_weight, down_weight):
    group_count = lax.axis_size("expert")
    tensor_count = lax.axis_size("tensor")
    tok_rows = tokens.shape[0]
    local_experts = EXP_DEV
    all_experts = local_experts * group_count
    top_count = routes.shape[1]
    capacity = tok_rows * top_count * 4 // (3 * all_experts)
    model_width = tokens.shape[1] * tensor_count
    unit_rows = gate_weight.shape[1]
    per_expert = HID // unit_rows
    owner = lax.axis_index("tensor") // per_expert
    dispatch, slot_gate = slot_tables(routes, route_gates, all_experts, capacity)
    whole_tokens, whole_grad = (
        lax.all_gather(tokens, "tensor", axis=1, tiled=True),
        lax.all_gather(out_grad, "tensor", axis=1, tiled=True),
    )
    send_rows = jnp.dot(dispatch, whole_tokens, preferred_element_type=jnp.float32).astype(
        jnp.bfloat16
    )
    send_scaled = (
        slot_gate * jnp.dot(dispatch, whole_grad, preferred_element_type=jnp.float32)
    ).astype(jnp.bfloat16)
    rows_x, rows_e = (
        lax.all_to_all(send_rows, "expert", split_axis=0, concat_axis=0, tiled=True),
        lax.all_to_all(send_scaled, "expert", split_axis=0, concat_axis=0, tiled=True),
    )
    shaped_x = rows_x.reshape(group_count, local_experts, capacity, model_width)
    shaped_e = rows_e.reshape(group_count, local_experts, capacity, model_width)
    mine_x = lax.dynamic_index_in_dim(shaped_x, owner, 1, keepdims=False)
    mine_e = lax.dynamic_index_in_dim(shaped_e, owner, 1, keepdims=False)
    gate_w = gate_weight[0]
    up_w = up_weight[0]
    down_w = down_weight[0]
    gate_pre = jnp.einsum("scd,hd->sch", mine_x, gate_w, preferred_element_type=jnp.float32)
    up_pre = jnp.einsum("scd,hd->sch", mine_x, up_w, preferred_element_type=jnp.float32)
    sigmoid_gate = jax.nn.sigmoid(gate_pre)
    activated = gate_pre * sigmoid_gate
    hidden = (activated * up_pre).astype(jnp.bfloat16)
    dhidden = jnp.einsum("scd,hd->sch", mine_e, down_w, preferred_element_type=jnp.float32)
    grad_down = jnp.einsum(
        "sch,scd->hd", hidden, mine_e, preferred_element_type=jnp.float32
    ).astype(jnp.bfloat16)
    grad_pre_gate = (
        dhidden * up_pre * sigmoid_gate * (1.0 + gate_pre * (1.0 - sigmoid_gate))
    ).astype(jnp.bfloat16)
    grad_pre_up = (dhidden * activated).astype(jnp.bfloat16)
    grad_gate = jnp.einsum(
        "sch,scd->hd", grad_pre_gate, mine_x, preferred_element_type=jnp.float32
    ).astype(jnp.bfloat16)
    grad_up = jnp.einsum(
        "sch,scd->hd", grad_pre_up, mine_x, preferred_element_type=jnp.float32
    ).astype(jnp.bfloat16)
    select = (jnp.arange(local_experts, dtype=jnp.int32) == owner).astype(jnp.float32)
    share_rows = model_width // tensor_count
    summed = jnp.einsum("hd,sch->dsc", gate_w, grad_pre_gate, preferred_element_type=jnp.float32)
    summed = summed + jnp.einsum(
        "hd,sch->dsc", up_w, grad_pre_up, preferred_element_type=jnp.float32
    )
    placed_term = summed[:, :, None, :] * select[None, None, :, None]
    reduced = lax.psum_scatter(
        placed_term.reshape(lax.axis_size("tensor") * share_rows, -1).astype(jnp.bfloat16),
        "tensor",
        scatter_dimension=0,
        tiled=True,
    )
    returned = lax.all_to_all(reduced, "expert", split_axis=1, concat_axis=1, tiled=True)
    in_grad = lax.dot_general(
        dispatch, returned, (((0,), (1,)), ((), ())), preferred_element_type=jnp.float32
    ).astype(jnp.bfloat16)
    return (in_grad, grad_gate[None], grad_up[None], grad_down[None])


def swap(value, axis, bit):
    count = lax.axis_size(axis)
    return lax.ppermute(value, axis, [(i, i ^ bit) for i in range(count)])


def gather_tensor(part):
    count = lax.axis_size("tensor")
    me = lax.axis_index("tensor")
    rows, width = part.shape
    whole = jnp.zeros((count, rows, width), part.dtype)
    whole = lax.dynamic_update_index_in_dim(whole, part, me, 0)
    for k in range(1, count):
        whole = lax.dynamic_update_index_in_dim(whole, swap(part, "tensor", k), me ^ k, 0)
    return jnp.swapaxes(whole, 0, 1).reshape(rows, count * width)


def gather_expert(block):
    half = block.shape[0] // 2
    far_x = swap(block, "expert", 2)
    far_y = swap(block, "expert", 4)
    diag = jnp.concatenate([swap(far_y[:half], "expert", 2), swap(far_x[half:], "expert", 4)], axis=0)
    mine = jnp.stack([block, far_x, far_y, diag])
    other = swap(mine, "expert", 1)
    return jnp.stack([mine, other], axis=1).reshape((8,) + block.shape)


def gather_shards(tokens, out_grad, routes, route_gates, gate_weight, up_weight, down_weight):
    bf16, f32 = jnp.bfloat16, jnp.float32
    group_count = lax.axis_size("expert")
    tensor_count = lax.axis_size("tensor")
    tok_rows = tokens.shape[0]
    all_experts = EXP_DEV * group_count
    capacity = tok_rows * routes.shape[1] * 4 // (3 * all_experts)
    width = tokens.shape[1]
    unit_rows = gate_weight.shape[1]
    owner = lax.axis_index("tensor") // (HID // unit_rows)
    me_t = lax.axis_index("tensor")
    expert = EXP_DEV * lax.axis_index("expert") + owner

    expert_ids = jnp.arange(all_experts, dtype=jnp.int32)
    named = routes[:, :, None] == expert_ids[None, None, :]
    table = jnp.where(
        jnp.any(named, axis=1),
        jnp.sum(jnp.where(named, route_gates[:, :, None], f32(0.0)), axis=1),
        f32(-1.0),
    ).T[None]
    for bit in (1, 2, 4):
        table = jnp.concatenate([table, swap(table, "expert", bit)], axis=0)
    gates = lax.dynamic_index_in_dim(table, expert, 1, keepdims=False)
    hit = gates >= 0.0
    hit_i = hit.astype(jnp.int32)
    rank = jnp.cumsum(hit_i, axis=1) - hit_i
    slot_ids = jnp.arange(capacity, dtype=jnp.int32)
    placed = (rank[:, None, :] == slot_ids[None, :, None]) & hit[:, None, :]
    slot_gate = jnp.sum(jnp.where(placed, gates[:, None, :], f32(0.0)), axis=2)
    pick = placed.astype(bf16)

    all_x = gather_expert(gather_tensor(tokens))
    all_e = gather_expert(gather_tensor(out_grad))
    rows_x = jnp.einsum("kst,ktd->ksd", pick, all_x, preferred_element_type=f32).astype(bf16)
    rows_e = (
        slot_gate[:, :, None] * jnp.einsum("kst,ktd->ksd", pick, all_e, preferred_element_type=f32)
    ).astype(bf16)
    gate_w, up_w, down_w = gate_weight[0], up_weight[0], down_weight[0]
    gate_pre = jnp.einsum("ksd,hd->ksh", rows_x, gate_w, preferred_element_type=f32)
    up_pre = jnp.einsum("ksd,hd->ksh", rows_x, up_w, preferred_element_type=f32)
    sigmoid_gate = jax.nn.sigmoid(gate_pre)
    activated = gate_pre * sigmoid_gate
    hidden = (activated * up_pre).astype(bf16)
    dhidden = jnp.einsum("ksd,hd->ksh", rows_e, down_w, preferred_element_type=f32)
    grad_pre_gate = (
        dhidden * up_pre * sigmoid_gate * (1.0 + gate_pre * (1.0 - sigmoid_gate))
    ).astype(bf16)
    grad_pre_up = (dhidden * activated).astype(bf16)
    grad_down = jnp.einsum("ksh,ksd->hd", hidden, rows_e, preferred_element_type=f32).astype(bf16)
    grad_gate = jnp.einsum("ksh,ksd->hd", grad_pre_gate, rows_x, preferred_element_type=f32).astype(bf16)
    grad_up = jnp.einsum("ksh,ksd->hd", grad_pre_up, rows_x, preferred_element_type=f32).astype(bf16)

    summed = jnp.einsum("ksh,hd->ksd", grad_pre_gate, gate_w, preferred_element_type=f32)
    summed = (summed + jnp.einsum("ksh,hd->ksd", grad_pre_up, up_w, preferred_element_type=f32)).astype(bf16)
    spread = jnp.einsum("kst,ksd->ktd", pick, summed, preferred_element_type=f32).astype(bf16)
    spread = spread.reshape(4, 2, tok_rows, -1)
    joined = (spread[:, 0].astype(f32) + swap(spread[:, 1], "expert", 1).astype(f32)).astype(bf16)
    half = tok_rows // 2
    via_x = swap(joined[3, :half], "expert", 2)
    via_y = swap(joined[3, half:], "expert", 4)
    pad = jnp.zeros_like(via_x)
    to_y = (joined[2].astype(f32) + jnp.concatenate([via_x, pad], axis=0).astype(f32)).astype(bf16)
    to_x = (joined[1].astype(f32) + jnp.concatenate([pad, via_y], axis=0).astype(f32)).astype(bf16)
    plane = (
        joined[0].astype(f32) + swap(to_x, "expert", 2).astype(f32) + swap(to_y, "expert", 4).astype(f32)
    ).astype(bf16).reshape(tok_rows, tensor_count, width)
    total = lax.dynamic_index_in_dim(plane, me_t, 1, keepdims=False).astype(f32)
    for k in range(1, tensor_count):
        total = total + swap(
            lax.dynamic_index_in_dim(plane, me_t ^ k, 1, keepdims=False), "tensor", k
        ).astype(f32)
    return (total.astype(bf16), grad_gate[None], grad_up[None], grad_down[None])


def solution(mesh):
    in_specs = (
        P("expert", "tensor"),
        P("expert", "tensor"),
        P("expert", None),
        P("expert", None),
        P("expert", "tensor", None),
        P("expert", "tensor", None),
        P("expert", "tensor", None),
    )
    out_specs = (
        P("expert", "tensor"),
        P("expert", "tensor", None),
        P("expert", "tensor", None),
        P("expert", "tensor", None),
    )
    groups, tensors = mesh.shape["expert"], mesh.shape["tensor"]
    gathers = groups == 8 and tensors & (tensors - 1) == 0
    shards = gather_shards if gathers else dispatch_shards
    return jax.shard_map(shards, mesh=mesh, in_specs=in_specs, out_specs=out_specs, check_vma=False)
```

```python
import functools

import jax
import jax.numpy as jnp
from jax import lax
from jax.experimental import pallas as pl
from jax.experimental.pallas import tpu as pltpu
from jax.sharding import PartitionSpec as P

HID = 1408
EXP_DEV = 2


def slot_tables(routes, route_gates, all_experts, capacity):
    expert_ids = jnp.arange(all_experts, dtype=jnp.int32)
    named_hit = routes[:, :, None] == expert_ids[None, None, :]
    hit_table = jnp.any(named_hit, axis=1).astype(jnp.int32)
    rank_table = jnp.cumsum(hit_table, axis=0) - hit_table
    gate_table = jnp.sum(jnp.where(named_hit, route_gates[:, :, None], jnp.float32(0.0)), axis=1)
    slot_ids = jnp.arange(capacity, dtype=jnp.int32)
    placed = (rank_table.T[:, None, :] == slot_ids[None, :, None]) & (hit_table.T[:, None, :] == 1)
    slot_gate = jnp.sum(jnp.where(placed, gate_table.T[:, None, :], jnp.float32(0.0)), axis=2)
    tok_rows = routes.shape[0]
    dispatch = placed.reshape(all_experts * capacity, tok_rows).astype(jnp.bfloat16)
    return (dispatch, slot_gate.reshape(all_experts * capacity, 1))


def dispatch_shards(tokens, out_grad, routes, route_gates, gate_weight, up_weight, down_weight):
    group_count = lax.axis_size("expert")
    tensor_count = lax.axis_size("tensor")
    tok_rows = tokens.shape[0]
    local_experts = EXP_DEV
    all_experts = local_experts * group_count
    top_count = routes.shape[1]
    capacity = tok_rows * top_count * 4 // (3 * all_experts)
    model_width = tokens.shape[1] * tensor_count
    unit_rows = gate_weight.shape[1]
    per_expert = HID // unit_rows
    owner = lax.axis_index("tensor") // per_expert
    dispatch, slot_gate = slot_tables(routes, route_gates, all_experts, capacity)
    whole_tokens, whole_grad = (
        lax.all_gather(tokens, "tensor", axis=1, tiled=True),
        lax.all_gather(out_grad, "tensor", axis=1, tiled=True),
    )
    send_rows = jnp.dot(dispatch, whole_tokens, preferred_element_type=jnp.float32).astype(
        jnp.bfloat16
    )
    send_scaled = (
        slot_gate * jnp.dot(dispatch, whole_grad, preferred_element_type=jnp.float32)
    ).astype(jnp.bfloat16)
    rows_x, rows_e = (
        lax.all_to_all(send_rows, "expert", split_axis=0, concat_axis=0, tiled=True),
        lax.all_to_all(send_scaled, "expert", split_axis=0, concat_axis=0, tiled=True),
    )
    shaped_x = rows_x.reshape(group_count, local_experts, capacity, model_width)
    shaped_e = rows_e.reshape(group_count, local_experts, capacity, model_width)
    mine_x = lax.dynamic_index_in_dim(shaped_x, owner, 1, keepdims=False)
    mine_e = lax.dynamic_index_in_dim(shaped_e, owner, 1, keepdims=False)
    gate_w = gate_weight[0]
    up_w = up_weight[0]
    down_w = down_weight[0]
    gate_pre = jnp.einsum("scd,hd->sch", mine_x, gate_w, preferred_element_type=jnp.float32)
    up_pre = jnp.einsum("scd,hd->sch", mine_x, up_w, preferred_element_type=jnp.float32)
    sigmoid_gate = jax.nn.sigmoid(gate_pre)
    activated = gate_pre * sigmoid_gate
    hidden = (activated * up_pre).astype(jnp.bfloat16)
    dhidden = jnp.einsum("scd,hd->sch", mine_e, down_w, preferred_element_type=jnp.float32)
    grad_down = jnp.einsum(
        "sch,scd->hd", hidden, mine_e, preferred_element_type=jnp.float32
    ).astype(jnp.bfloat16)
    grad_pre_gate = (
        dhidden * up_pre * sigmoid_gate * (1.0 + gate_pre * (1.0 - sigmoid_gate))
    ).astype(jnp.bfloat16)
    grad_pre_up = (dhidden * activated).astype(jnp.bfloat16)
    grad_gate = jnp.einsum(
        "sch,scd->hd", grad_pre_gate, mine_x, preferred_element_type=jnp.float32
    ).astype(jnp.bfloat16)
    grad_up = jnp.einsum(
        "sch,scd->hd", grad_pre_up, mine_x, preferred_element_type=jnp.float32
    ).astype(jnp.bfloat16)
    select = (jnp.arange(local_experts, dtype=jnp.int32) == owner).astype(jnp.float32)
    share_rows = model_width // tensor_count
    summed = jnp.einsum("hd,sch->dsc", gate_w, grad_pre_gate, preferred_element_type=jnp.float32)
    summed = summed + jnp.einsum(
        "hd,sch->dsc", up_w, grad_pre_up, preferred_element_type=jnp.float32
    )
    placed_term = summed[:, :, None, :] * select[None, None, :, None]
    reduced = lax.psum_scatter(
        placed_term.reshape(lax.axis_size("tensor") * share_rows, -1).astype(jnp.bfloat16),
        "tensor",
        scatter_dimension=0,
        tiled=True,
    )
    returned = lax.all_to_all(reduced, "expert", split_axis=1, concat_axis=1, tiled=True)
    in_grad = lax.dot_general(
        dispatch, returned, (((0,), (1,)), ((), ())), preferred_element_type=jnp.float32
    ).astype(jnp.bfloat16)
    return (in_grad, grad_gate[None], grad_up[None], grad_down[None])

bf16, f32 = jnp.bfloat16, jnp.float32
ANY = pl.BlockSpec(memory_space=pl.ANY)
NT = (((1,), (1,)), ((), ()))
TN = (((0,), (0,)), ((), ()))


def swap(value, axis, bit):
    count = lax.axis_size(axis)
    return lax.ppermute(value, axis, [(i, i ^ bit) for i in range(count)])


def dot(a, b, dims=(((1,), (0,)), ((), ()))):
    return lax.dot_general(a, b, dims, preferred_element_type=f32)


def tiles_of(size, step=256):
    return [(at, min(step, size - at)) for at in range(0, size, step)]


def picks(gates_ref, capacity):
    gates = gates_ref[...]
    blocks, tok_rows = gates.shape
    hit = (gates >= 0.0).astype(f32)
    before = lax.broadcasted_iota(jnp.int32, (tok_rows, tok_rows), 0) < lax.broadcasted_iota(
        jnp.int32, (tok_rows, tok_rows), 1
    )
    rank = dot(hit.astype(bf16), before.astype(f32).astype(bf16))
    slots = lax.broadcasted_iota(jnp.int32, (capacity, tok_rows), 0).astype(f32)

    def one(k):
        chosen = jnp.where(slots == rank[k : k + 1], hit[k : k + 1], 0.0)
        gate = jnp.sum(chosen * jnp.maximum(gates[k : k + 1], 0.0), axis=1, keepdims=True)
        return chosen.astype(bf16), gate

    return one


def forward_kernel(capacity, parts, width, me_ref, gates_ref, *refs):
    blocks = len(parts)
    count = sum(parts)
    pieces, (gate_hbm, up_hbm) = refs[:count], refs[count : count + 2]
    rows_hbm, hidden_hbm, act_hbm, slope_hbm = refs[count + 2 : count + 6]
    scratch = refs[count + 6 :]
    held, (gate_w, up_w, rows, hidden, act, slope, sems, out_sems) = scratch[:count], scratch[count:]
    loads = [pltpu.make_async_copy(p, h, sems.at[i]) for i, (p, h) in enumerate(zip(pieces, held))]
    loads.append(pltpu.make_async_copy(gate_hbm, gate_w, sems.at[count]))
    loads.append(pltpu.make_async_copy(up_hbm, up_w, sems.at[count + 1]))
    for load in loads:
        load.start()
    pick = picks(gates_ref, capacity)
    at = 0
    for k in range(blocks):
        chosen, _ = pick(k)
        s = 0
        for piece in range(at, at + parts[k]):
            loads[piece].wait()
            for i in range(held[piece].shape[0]):
                column = pl.multiple_of((me_ref[0] ^ s) * width, width)
                rows[pl.ds(k * capacity, capacity), pl.ds(column, width)] = dot(
                    chosen, held[piece][i]
                ).astype(bf16)
                s += 1
        at += parts[k]
    stores = [pltpu.make_async_copy(rows, rows_hbm, out_sems.at[0])]
    stores[0].start()
    loads[count].wait()
    loads[count + 1].wait()
    for start, size in tiles_of(gate_w.shape[0]):
        span = pl.ds(start, size)
        gate_pre = dot(rows[...], gate_w[span, :], NT)
        up_pre = dot(rows[...], up_w[span, :], NT)
        sigmoid_gate = jax.nn.sigmoid(gate_pre)
        activated = gate_pre * sigmoid_gate
        act[:, span] = activated
        hidden[:, span] = (activated * up_pre).astype(bf16)
        slope[:, span] = up_pre * sigmoid_gate * (1.0 + gate_pre * (1.0 - sigmoid_gate))
    for i, (value, target) in enumerate(((hidden, hidden_hbm), (act, act_hbm), (slope, slope_hbm))):
        stores.append(pltpu.make_async_copy(value, target, out_sems.at[i + 1]))
        stores[-1].start()
    for store in stores:
        store.wait()


def forward(capacity, me, gates, blocks, gate_w, up_w):
    parts = tuple(len(b) for b in blocks)
    pieces = [p for b in blocks for p in b]
    width = pieces[0].shape[-1]
    slots = capacity * len(blocks)
    units, model = gate_w.shape
    count = len(pieces)
    return pl.pallas_call(
        functools.partial(forward_kernel, capacity, parts, width),
        out_shape=(
            jax.ShapeDtypeStruct((slots, model), bf16),
            jax.ShapeDtypeStruct((slots, units), bf16),
            jax.ShapeDtypeStruct((slots, units), f32),
            jax.ShapeDtypeStruct((slots, units), f32),
        ),
        in_specs=[pl.BlockSpec(memory_space=pltpu.SMEM), pl.BlockSpec(memory_space=pltpu.VMEM)]
        + [ANY] * (count + 2),
        out_specs=(ANY,) * 4,
        scratch_shapes=[pltpu.VMEM(p.shape, bf16) for p in pieces]
        + [
            pltpu.VMEM((units, model), bf16),
            pltpu.VMEM((units, model), bf16),
            pltpu.VMEM((slots, model), bf16),
            pltpu.VMEM((slots, units), bf16),
            pltpu.VMEM((slots, units), f32),
            pltpu.VMEM((slots, units), f32),
            pltpu.SemaphoreType.DMA((count + 2,)),
            pltpu.SemaphoreType.DMA((4,)),
        ],
        cost_estimate=pl.CostEstimate(
            flops=4 * slots * units * model, bytes_accessed=4 * units * model, transcendentals=0
        ),
        name="forward",
    )(me, gates, *pieces, gate_w, up_w)


def backward_kernel(capacity, first, parts, width, fresh, me_ref, gates_ref, *refs):
    blocks, count = len(parts), sum(parts)
    pieces, refs = refs[:count], refs[count:]
    act_hbm, slope_hbm, down_hbm, gate_hbm, up_hbm = refs[:5]
    refs = refs[5:] if fresh else refs[8:]
    rows_hbm, grad_gate_hbm, grad_up_hbm, even_hbm, odd_hbm = refs[:5]
    refs = refs[5:]
    held, refs = refs[:count], refs[count:]
    down_w, gate_w, up_w, rows, act, slope, grad_gate, grad_up, even, odd, sems, out_sems = refs
    mine = pl.ds(first * capacity, blocks * capacity)
    loads = [pltpu.make_async_copy(p, h, sems.at[i]) for i, (p, h) in enumerate(zip(pieces, held))]
    for source, target in (
        (down_hbm, down_w),
        (act_hbm.at[mine], act),
        (slope_hbm.at[mine], slope),
        (gate_hbm, gate_w),
        (up_hbm, up_w),
    ):
        loads.append(pltpu.make_async_copy(source, target, sems.at[len(loads)]))
    for load in loads:
        load.start()
    pick = picks(gates_ref, capacity)
    chosen = []
    at = 0
    for k in range(blocks):
        one, gate = pick(first + k)
        chosen.append(one)
        s = 0
        for piece in range(at, at + parts[k]):
            loads[piece].wait()
            for i in range(held[piece].shape[0]):
                column = pl.multiple_of((me_ref[0] ^ s) * width, width)
                rows[pl.ds(k * capacity, capacity), pl.ds(column, width)] = (
                    gate * dot(one, held[piece][i])
                ).astype(bf16)
                s += 1
        at += parts[k]
    stores = [pltpu.make_async_copy(rows, rows_hbm.at[mine], out_sems.at[0])]
    stores[0].start()
    for load in loads[count : count + 3]:
        load.wait()
    for start, size in tiles_of(down_w.shape[0]):
        span = pl.ds(start, size)
        dhidden = dot(rows[...], down_w[span, :], NT)
        grad_gate[:, span] = (dhidden * slope[:, span]).astype(bf16)
        grad_up[:, span] = (dhidden * act[:, span]).astype(bf16)
    stores.append(pltpu.make_async_copy(grad_gate, grad_gate_hbm.at[mine], out_sems.at[1]))
    stores.append(pltpu.make_async_copy(grad_up, grad_up_hbm.at[mine], out_sems.at[2]))
    stores[1].start()
    stores[2].start()
    for load in loads[count + 3 :]:
        load.wait()

    for s in range(4):
        column = pl.ds(pl.multiple_of((me_ref[0] ^ s) * width, width), width)
        summed = (
            dot(grad_gate[...], gate_w[:, column]) + dot(grad_up[...], up_w[:, column])
        ).astype(bf16)
        for k in range(blocks):
            target = even if k % 2 == 0 else odd
            target[k // 2, s] = dot(
                chosen[k], summed[k * capacity : (k + 1) * capacity], TN
            ).astype(bf16)
    stores.append(pltpu.make_async_copy(even, even_hbm, out_sems.at[3]))
    stores.append(pltpu.make_async_copy(odd, odd_hbm, out_sems.at[4]))
    stores[3].start()
    stores[4].start()
    for store in stores:
        store.wait()


def backward(capacity, first, me, gates, blocks, act, slope, down_w, gate_w, up_w, earlier=()):
    parts = tuple(len(b) for b in blocks)
    pieces = [p for b in blocks for p in b]
    width = pieces[0].shape[-1]
    tok_rows = pieces[0].shape[-2]
    slots = capacity * len(blocks)
    all_slots = act.shape[0]
    units, model = gate_w.shape
    count = len(pieces)
    half = jax.ShapeDtypeStruct((len(blocks) // 2, model // width, tok_rows, width), bf16)
    return pl.pallas_call(
        functools.partial(backward_kernel, capacity, first, parts, width, not earlier),
        out_shape=(
            jax.ShapeDtypeStruct((all_slots, model), bf16),
            jax.ShapeDtypeStruct((all_slots, units), bf16),
            jax.ShapeDtypeStruct((all_slots, units), bf16),
            half,
            half,
        ),
        in_specs=[pl.BlockSpec(memory_space=pltpu.SMEM), pl.BlockSpec(memory_space=pltpu.VMEM)]
        + [ANY] * (count + 5 + len(earlier)),
        out_specs=(ANY,) * 5,
        scratch_shapes=[pltpu.VMEM(p.shape, bf16) for p in pieces]
        + [pltpu.VMEM((units, model), bf16)] * 3
        + [
            pltpu.VMEM((slots, model), bf16),
            pltpu.VMEM((slots, units), f32),
            pltpu.VMEM((slots, units), f32),
            pltpu.VMEM((slots, units), bf16),
            pltpu.VMEM((slots, units), bf16),
            pltpu.VMEM(half.shape, bf16),
            pltpu.VMEM(half.shape, bf16),
            pltpu.SemaphoreType.DMA((count + 5,)),
            pltpu.SemaphoreType.DMA((5,)),
        ],
        input_output_aliases={2 + count + 5 + i: i for i in range(len(earlier))},
        cost_estimate=pl.CostEstimate(
            flops=6 * slots * units * model, bytes_accessed=6 * units * model, transcendentals=0
        ),
        name="backward",
    )(me, gates, *pieces, act, slope, down_w, gate_w, up_w, *earlier)


def join(*values):
    return functools.reduce(lambda a, b: a + b, [v.astype(f32) for v in values])


def gather_shards(tokens, out_grad, routes, route_gates, gate_weight, up_weight, down_weight):
    group_count = lax.axis_size("expert")
    tok_rows = tokens.shape[0]
    all_experts = EXP_DEV * group_count
    capacity = tok_rows * routes.shape[1] * 4 // (3 * all_experts)
    unit_rows = gate_weight.shape[1]
    me_t = lax.axis_index("tensor")
    expert = EXP_DEV * lax.axis_index("expert") + me_t // (HID // unit_rows)
    gate_w, up_w, down_w = gate_weight[0], up_weight[0], down_weight[0]

    def slices(part):
        near = jnp.stack([part, swap(part, "tensor", 1)])
        second = swap(part, "tensor", 2)
        far = jnp.stack([second, swap(second, "tensor", 1)])
        return near, far

    x_near, x_far = slices(tokens)
    x_own = [x_near, x_far]
    x_x = [swap(p, "expert", 2) for p in x_own]
    x_y = [swap(p, "expert", 4) for p in x_own]
    x_d = [swap(x_y[0], "expert", 2), swap(x_x[1], "expert", 4)]
    x_blocks = []
    for block in (x_own, x_x, x_y, x_d):
        x_blocks += [block, [swap(p, "expert", 1) for p in block]]

    e_near, e_far = slices(out_grad)
    e_own = jnp.concatenate([e_near, e_far], axis=0)
    e_x, e_y = swap(e_own, "expert", 2), swap(e_own, "expert", 4)
    e_d = [swap(e_y[:2], "expert", 2), swap(e_x[2:], "expert", 4)]
    e_blocks = []
    for block in ([e_own], [e_x], [e_y], e_d):
        e_blocks += [block, [swap(p, "expert", 1) for p in block]]

    expert_ids = jnp.arange(all_experts, dtype=jnp.int32)
    named = routes[:, :, None] == expert_ids[None, None, :]
    table = jnp.where(
        jnp.any(named, axis=1),
        jnp.sum(jnp.where(named, route_gates[:, :, None], f32(0.0)), axis=1),
        f32(-1.0),
    ).T[None]
    for bit in (1, 2, 4):
        table = jnp.concatenate([table, swap(table, "expert", bit)], axis=0)
    gates = lax.dynamic_index_in_dim(table, expert, 1, keepdims=False)
    me = me_t.astype(jnp.int32).reshape(1)

    rows_x, hidden, act, slope = forward(capacity, me, gates, x_blocks, gate_w, up_w)
    first = backward(capacity, 0, me, gates, e_blocks[:6], act, slope, down_w, gate_w, up_w)
    second = backward(
        capacity, 6, me, gates, e_blocks[6:], act, slope, down_w, gate_w, up_w, first[:3]
    )
    rows_e, grad_pre_gate, grad_pre_up, keep_d, give_d = second
    keep, give = first[3:]

    got_d = swap(give_d, "expert", 1)
    got = swap(give, "expert", 1)
    diag_near = join(keep_d[0, :2], got_d[0, :2]).astype(bf16)
    diag_far = join(keep_d[0, 2:], got_d[0, 2:]).astype(bf16)
    relay_near = swap(diag_near, "expert", 2)
    relay_far = swap(diag_far, "expert", 4)
    far_x = swap(join(keep[1, 2:], got[1, 2:], relay_far).astype(bf16), "expert", 2)
    far_y = swap(join(keep[2, 2:], got[2, 2:]).astype(bf16), "expert", 4)
    near_x = swap(join(keep[1, :2], got[1, :2]).astype(bf16), "expert", 2)
    near_y = swap(join(keep[2, :2], got[2, :2], relay_near).astype(bf16), "expert", 4)
    far = join(keep[0, 2:], got[0, 2:], far_x, far_y)
    near = join(keep[0, :2], got[0, :2], near_x, near_y)
    third = swap(far[1].astype(bf16), "tensor", 1)
    second_z = swap(join(far[0], third).astype(bf16), "tensor", 2)
    first_z = swap(near[1].astype(bf16), "tensor", 1)
    in_grad = join(near[0], first_z, second_z).astype(bf16)

    def weight_grad(left, right):
        return lax.dot_general(left, right, TN, preferred_element_type=f32).astype(bf16)[None]

    return (
        in_grad,
        weight_grad(grad_pre_gate, rows_x),
        weight_grad(grad_pre_up, rows_x),
        weight_grad(hidden, rows_e),
    )


def solution(mesh):
    in_specs = (
        P("expert", "tensor"),
        P("expert", "tensor"),
        P("expert", None),
        P("expert", None),
        P("expert", "tensor", None),
        P("expert", "tensor", None),
        P("expert", "tensor", None),
    )
    out_specs = (
        P("expert", "tensor"),
        P("expert", "tensor", None),
        P("expert", "tensor", None),
        P("expert", "tensor", None),
    )
    groups, tensors = mesh.shape["expert"], mesh.shape["tensor"]
    shards = gather_shards if (groups, tensors) == (8, 4) else dispatch_shards
    return jax.shard_map(shards, mesh=mesh, in_specs=in_specs, out_specs=out_specs, check_vma=False)
```

```python
import functools

import jax
import jax.numpy as jnp
from jax import lax
from jax.experimental import pallas as pl
from jax.experimental.pallas import tpu as pltpu
from jax.sharding import PartitionSpec as P

HID = 1408
EXP_DEV = 2


def slot_tables(routes, route_gates, all_experts, capacity):
    expert_ids = jnp.arange(all_experts, dtype=jnp.int32)
    named_hit = routes[:, :, None] == expert_ids[None, None, :]
    hit_table = jnp.any(named_hit, axis=1).astype(jnp.int32)
    rank_table = jnp.cumsum(hit_table, axis=0) - hit_table
    gate_table = jnp.sum(jnp.where(named_hit, route_gates[:, :, None], jnp.float32(0.0)), axis=1)
    slot_ids = jnp.arange(capacity, dtype=jnp.int32)
    placed = (rank_table.T[:, None, :] == slot_ids[None, :, None]) & (hit_table.T[:, None, :] == 1)
    slot_gate = jnp.sum(jnp.where(placed, gate_table.T[:, None, :], jnp.float32(0.0)), axis=2)
    tok_rows = routes.shape[0]
    dispatch = placed.reshape(all_experts * capacity, tok_rows).astype(jnp.bfloat16)
    return (dispatch, slot_gate.reshape(all_experts * capacity, 1))


def dispatch_shards(tokens, out_grad, routes, route_gates, gate_weight, up_weight, down_weight):
    group_count = lax.axis_size("expert")
    tensor_count = lax.axis_size("tensor")
    tok_rows = tokens.shape[0]
    local_experts = EXP_DEV
    all_experts = local_experts * group_count
    top_count = routes.shape[1]
    capacity = tok_rows * top_count * 4 // (3 * all_experts)
    model_width = tokens.shape[1] * tensor_count
    unit_rows = gate_weight.shape[1]
    per_expert = HID // unit_rows
    owner = lax.axis_index("tensor") // per_expert
    dispatch, slot_gate = slot_tables(routes, route_gates, all_experts, capacity)
    whole_tokens, whole_grad = (
        lax.all_gather(tokens, "tensor", axis=1, tiled=True),
        lax.all_gather(out_grad, "tensor", axis=1, tiled=True),
    )
    send_rows = jnp.dot(dispatch, whole_tokens, preferred_element_type=jnp.float32).astype(
        jnp.bfloat16
    )
    send_scaled = (
        slot_gate * jnp.dot(dispatch, whole_grad, preferred_element_type=jnp.float32)
    ).astype(jnp.bfloat16)
    rows_x, rows_e = (
        lax.all_to_all(send_rows, "expert", split_axis=0, concat_axis=0, tiled=True),
        lax.all_to_all(send_scaled, "expert", split_axis=0, concat_axis=0, tiled=True),
    )
    shaped_x = rows_x.reshape(group_count, local_experts, capacity, model_width)
    shaped_e = rows_e.reshape(group_count, local_experts, capacity, model_width)
    mine_x = lax.dynamic_index_in_dim(shaped_x, owner, 1, keepdims=False)
    mine_e = lax.dynamic_index_in_dim(shaped_e, owner, 1, keepdims=False)
    gate_w = gate_weight[0]
    up_w = up_weight[0]
    down_w = down_weight[0]
    gate_pre = jnp.einsum("scd,hd->sch", mine_x, gate_w, preferred_element_type=jnp.float32)
    up_pre = jnp.einsum("scd,hd->sch", mine_x, up_w, preferred_element_type=jnp.float32)
    sigmoid_gate = jax.nn.sigmoid(gate_pre)
    activated = gate_pre * sigmoid_gate
    hidden = (activated * up_pre).astype(jnp.bfloat16)
    dhidden = jnp.einsum("scd,hd->sch", mine_e, down_w, preferred_element_type=jnp.float32)
    grad_down = jnp.einsum(
        "sch,scd->hd", hidden, mine_e, preferred_element_type=jnp.float32
    ).astype(jnp.bfloat16)
    grad_pre_gate = (
        dhidden * up_pre * sigmoid_gate * (1.0 + gate_pre * (1.0 - sigmoid_gate))
    ).astype(jnp.bfloat16)
    grad_pre_up = (dhidden * activated).astype(jnp.bfloat16)
    grad_gate = jnp.einsum(
        "sch,scd->hd", grad_pre_gate, mine_x, preferred_element_type=jnp.float32
    ).astype(jnp.bfloat16)
    grad_up = jnp.einsum(
        "sch,scd->hd", grad_pre_up, mine_x, preferred_element_type=jnp.float32
    ).astype(jnp.bfloat16)
    select = (jnp.arange(local_experts, dtype=jnp.int32) == owner).astype(jnp.float32)
    share_rows = model_width // tensor_count
    summed = jnp.einsum("hd,sch->dsc", gate_w, grad_pre_gate, preferred_element_type=jnp.float32)
    summed = summed + jnp.einsum(
        "hd,sch->dsc", up_w, grad_pre_up, preferred_element_type=jnp.float32
    )
    placed_term = summed[:, :, None, :] * select[None, None, :, None]
    reduced = lax.psum_scatter(
        placed_term.reshape(lax.axis_size("tensor") * share_rows, -1).astype(jnp.bfloat16),
        "tensor",
        scatter_dimension=0,
        tiled=True,
    )
    returned = lax.all_to_all(reduced, "expert", split_axis=1, concat_axis=1, tiled=True)
    in_grad = lax.dot_general(
        dispatch, returned, (((0,), (1,)), ((), ())), preferred_element_type=jnp.float32
    ).astype(jnp.bfloat16)
    return (in_grad, grad_gate[None], grad_up[None], grad_down[None])

bf16, f32 = jnp.bfloat16, jnp.float32
ANY = pl.BlockSpec(memory_space=pl.ANY)
HELD = pl.BlockSpec(memory_space=pltpu.VMEM)
VMEM_GRANT = 16 << 20


def held(*values):
    return [pltpu.with_memory_space_constraint(v, pltpu.VMEM) for v in values]


NT = (((1,), (1,)), ((), ()))
TN = (((0,), (0,)), ((), ()))


def swap(value, axis, bit):
    count = lax.axis_size(axis)
    return lax.ppermute(value, axis, [(i, i ^ bit) for i in range(count)])


def dot(a, b, dims=(((1,), (0,)), ((), ()))):
    return lax.dot_general(a, b, dims, preferred_element_type=f32)


def tiles_of(size, step=256):
    return [(at, min(step, size - at)) for at in range(0, size, step)]


def picks(gates_ref, capacity):
    gates = gates_ref[...]
    blocks, tok_rows = gates.shape
    hit = (gates >= 0.0).astype(f32)
    before = lax.broadcasted_iota(jnp.int32, (tok_rows, tok_rows), 0) < lax.broadcasted_iota(
        jnp.int32, (tok_rows, tok_rows), 1
    )
    rank = dot(hit.astype(bf16), before.astype(f32).astype(bf16))
    slots = lax.broadcasted_iota(jnp.int32, (capacity, tok_rows), 0).astype(f32)

    def one(k):
        chosen = jnp.where(slots == rank[k : k + 1], hit[k : k + 1], 0.0)
        gate = jnp.sum(chosen * jnp.maximum(gates[k : k + 1], 0.0), axis=1, keepdims=True)
        return chosen.astype(bf16), gate

    return one


def forward_kernel(capacity, parts, width, me_ref, gates_ref, *refs):
    blocks = len(parts)
    count = sum(parts)
    held, (gate_w, up_w, rows_hbm, hidden_hbm, act, slope, rows, hidden, out_sems) = (
        refs[:count],
        refs[count:],
    )
    pick = picks(gates_ref, capacity)
    at = 0
    for k in range(blocks):
        chosen, _ = pick(k)
        s = 0
        for piece in range(at, at + parts[k]):
            for i in range(held[piece].shape[0]):
                column = pl.multiple_of((me_ref[0] ^ s) * width, width)
                rows[pl.ds(k * capacity, capacity), pl.ds(column, width)] = dot(
                    chosen, held[piece][i]
                ).astype(bf16)
                s += 1
        at += parts[k]
    stores = [pltpu.make_async_copy(rows, rows_hbm, out_sems.at[0])]
    stores[0].start()
    for start, size in tiles_of(gate_w.shape[0]):
        span = pl.ds(start, size)
        gate_pre = dot(rows[...], gate_w[span, :], NT)
        up_pre = dot(rows[...], up_w[span, :], NT)
        sigmoid_gate = jax.nn.sigmoid(gate_pre)
        activated = gate_pre * sigmoid_gate
        act[:, span] = activated
        hidden[:, span] = (activated * up_pre).astype(bf16)
        slope[:, span] = up_pre * sigmoid_gate * (1.0 + gate_pre * (1.0 - sigmoid_gate))
    stores.append(pltpu.make_async_copy(hidden, hidden_hbm, out_sems.at[1]))
    stores[1].start()
    for store in stores:
        store.wait()


def forward(capacity, me, gates, blocks, gate_w, up_w):
    parts = tuple(len(b) for b in blocks)
    pieces = [p for b in blocks for p in b]
    width = pieces[0].shape[-1]
    slots = capacity * len(blocks)
    units, model = gate_w.shape
    count = len(pieces)
    return pl.pallas_call(
        functools.partial(forward_kernel, capacity, parts, width),
        out_shape=(
            jax.ShapeDtypeStruct((slots, model), bf16),
            jax.ShapeDtypeStruct((slots, units), bf16),
            pltpu.VMEM((slots, units), f32),
            pltpu.VMEM((slots, units), f32),
        ),
        in_specs=[pl.BlockSpec(memory_space=pltpu.SMEM)] + [HELD] * (count + 3),
        out_specs=(ANY, ANY, HELD, HELD),
        scratch_shapes=[
            pltpu.VMEM((slots, model), bf16),
            pltpu.VMEM((slots, units), bf16),
            pltpu.SemaphoreType.DMA((2,)),
        ],
        compiler_params=pltpu.CompilerParams(vmem_limit_bytes=VMEM_GRANT),
        cost_estimate=pl.CostEstimate(
            flops=4 * slots * units * model, bytes_accessed=4 * units * model, transcendentals=0
        ),
        name="forward",
    )(me, gates, *held(*pieces, gate_w, up_w))


def backward_kernel(capacity, first, parts, width, fresh, me_ref, gates_ref, *refs):
    blocks, count = len(parts), sum(parts)
    held, refs = refs[:count], refs[count:]
    act, slope, down_w, gate_w, up_w = refs[:5]
    refs = refs[5:] if fresh else refs[8:]
    rows_hbm, grad_gate_hbm, grad_up_hbm, even_hbm, odd_hbm = refs[:5]
    rows, grad_gate, grad_up, even, odd, out_sems = refs[5:]
    mine = pl.ds(first * capacity, blocks * capacity)
    pick = picks(gates_ref, capacity)
    chosen = []
    at = 0
    for k in range(blocks):
        one, gate = pick(first + k)
        chosen.append(one)
        s = 0
        for piece in range(at, at + parts[k]):
            for i in range(held[piece].shape[0]):
                column = pl.multiple_of((me_ref[0] ^ s) * width, width)
                rows[pl.ds(k * capacity, capacity), pl.ds(column, width)] = (
                    gate * dot(one, held[piece][i])
                ).astype(bf16)
                s += 1
        at += parts[k]
    stores = [pltpu.make_async_copy(rows, rows_hbm.at[mine], out_sems.at[0])]
    stores[0].start()
    for start, size in tiles_of(down_w.shape[0]):
        span = pl.ds(start, size)
        dhidden = dot(rows[...], down_w[span, :], NT)
        grad_gate[:, span] = (dhidden * slope[mine, span]).astype(bf16)
        grad_up[:, span] = (dhidden * act[mine, span]).astype(bf16)
    stores.append(pltpu.make_async_copy(grad_gate, grad_gate_hbm.at[mine], out_sems.at[1]))
    stores.append(pltpu.make_async_copy(grad_up, grad_up_hbm.at[mine], out_sems.at[2]))
    stores[1].start()
    stores[2].start()
    for s in range(4):
        column = pl.ds(pl.multiple_of((me_ref[0] ^ s) * width, width), width)
        summed = (
            dot(grad_gate[...], gate_w[:, column]) + dot(grad_up[...], up_w[:, column])
        ).astype(bf16)
        for k in range(blocks):
            target = even if k % 2 == 0 else odd
            target[k // 2, s] = dot(
                chosen[k], summed[k * capacity : (k + 1) * capacity], TN
            ).astype(bf16)
    stores.append(pltpu.make_async_copy(even, even_hbm, out_sems.at[3]))
    stores.append(pltpu.make_async_copy(odd, odd_hbm, out_sems.at[4]))
    stores[3].start()
    stores[4].start()
    for store in stores:
        store.wait()


def backward(capacity, first, me, gates, blocks, act, slope, down_w, gate_w, up_w, earlier=()):
    parts = tuple(len(b) for b in blocks)
    pieces = [p for b in blocks for p in b]
    width = pieces[0].shape[-1]
    tok_rows = pieces[0].shape[-2]
    slots = capacity * len(blocks)
    all_slots = act.shape[0]
    units, model = gate_w.shape
    count = len(pieces)
    half = jax.ShapeDtypeStruct((len(blocks) // 2, model // width, tok_rows, width), bf16)
    return pl.pallas_call(
        functools.partial(backward_kernel, capacity, first, parts, width, not earlier),
        out_shape=(
            jax.ShapeDtypeStruct((all_slots, model), bf16),
            jax.ShapeDtypeStruct((all_slots, units), bf16),
            jax.ShapeDtypeStruct((all_slots, units), bf16),
            half,
            half,
        ),
        in_specs=[pl.BlockSpec(memory_space=pltpu.SMEM)] + [HELD] * (count + 6) + [ANY] * len(earlier),
        out_specs=(ANY,) * 5,
        scratch_shapes=[
            pltpu.VMEM((slots, model), bf16),
            pltpu.VMEM((slots, units), bf16),
            pltpu.VMEM((slots, units), bf16),
            pltpu.VMEM(half.shape, bf16),
            pltpu.VMEM(half.shape, bf16),
            pltpu.SemaphoreType.DMA((5,)),
        ],
        input_output_aliases={2 + count + 5 + i: i for i in range(len(earlier))},
        compiler_params=pltpu.CompilerParams(vmem_limit_bytes=VMEM_GRANT),
        cost_estimate=pl.CostEstimate(
            flops=6 * slots * units * model, bytes_accessed=6 * units * model, transcendentals=0
        ),
        name="backward",
    )(me, gates, *held(*pieces), act, slope, *held(down_w, gate_w, up_w), *earlier)


def join(*values):
    return functools.reduce(lambda a, b: a + b, [v.astype(f32) for v in values])


def gather_shards(tokens, out_grad, routes, route_gates, gate_weight, up_weight, down_weight):
    group_count = lax.axis_size("expert")
    tok_rows = tokens.shape[0]
    all_experts = EXP_DEV * group_count
    capacity = tok_rows * routes.shape[1] * 4 // (3 * all_experts)
    unit_rows = gate_weight.shape[1]
    me_t = lax.axis_index("tensor")
    expert = EXP_DEV * lax.axis_index("expert") + me_t // (HID // unit_rows)
    gate_w, up_w, down_w = gate_weight[0], up_weight[0], down_weight[0]

    def slices(part):
        near = jnp.stack([part, swap(part, "tensor", 1)])
        second = swap(part, "tensor", 2)
        far = jnp.stack([second, swap(second, "tensor", 1)])
        return near, far

    x_near, x_far = slices(tokens)
    x_own = [x_near, x_far]
    x_x = [swap(p, "expert", 2) for p in x_own]
    x_y = [swap(p, "expert", 4) for p in x_own]
    x_d = [swap(x_y[0], "expert", 2), swap(x_x[1], "expert", 4)]
    x_blocks = []
    for block in (x_own, x_x, x_y, x_d):
        x_blocks += [block, [swap(p, "expert", 1) for p in block]]

    e_near, e_far = slices(out_grad)
    e_own = jnp.concatenate([e_near, e_far], axis=0)
    e_x, e_y = swap(e_own, "expert", 2), swap(e_own, "expert", 4)
    e_d = [swap(e_y[:2], "expert", 2), swap(e_x[2:], "expert", 4)]
    e_blocks = []
    for block in ([e_own], [e_x], [e_y], e_d):
        e_blocks += [block, [swap(p, "expert", 1) for p in block]]

    expert_ids = jnp.arange(all_experts, dtype=jnp.int32)
    named = routes[:, :, None] == expert_ids[None, None, :]
    table = jnp.where(
        jnp.any(named, axis=1),
        jnp.sum(jnp.where(named, route_gates[:, :, None], f32(0.0)), axis=1),
        f32(-1.0),
    ).T[None]
    for bit in (1, 2, 4):
        table = jnp.concatenate([table, swap(table, "expert", bit)], axis=0)
    gates = lax.dynamic_index_in_dim(table, expert, 1, keepdims=False)
    me = me_t.astype(jnp.int32).reshape(1)

    rows_x, hidden, act, slope = forward(capacity, me, gates, x_blocks, gate_w, up_w)
    first = backward(capacity, 0, me, gates, e_blocks[:6], act, slope, down_w, gate_w, up_w)
    second = backward(
        capacity, 6, me, gates, e_blocks[6:], act, slope, down_w, gate_w, up_w, first[:3]
    )
    rows_e, grad_pre_gate, grad_pre_up, keep_d, give_d = second
    keep, give = first[3:]

    got_d = swap(give_d, "expert", 1)
    got = swap(give, "expert", 1)
    diag_near = join(keep_d[0, :2], got_d[0, :2]).astype(bf16)
    diag_far = join(keep_d[0, 2:], got_d[0, 2:]).astype(bf16)
    relay_near = swap(diag_near, "expert", 2)
    relay_far = swap(diag_far, "expert", 4)
    far_x = swap(join(keep[1, 2:], got[1, 2:], relay_far).astype(bf16), "expert", 2)
    far_y = swap(join(keep[2, 2:], got[2, 2:]).astype(bf16), "expert", 4)
    near_x = swap(join(keep[1, :2], got[1, :2]).astype(bf16), "expert", 2)
    near_y = swap(join(keep[2, :2], got[2, :2], relay_near).astype(bf16), "expert", 4)
    far = join(keep[0, 2:], got[0, 2:], far_x, far_y)
    near = join(keep[0, :2], got[0, :2], near_x, near_y)
    third = swap(far[1].astype(bf16), "tensor", 1)
    second_z = swap(join(far[0], third).astype(bf16), "tensor", 2)
    first_z = swap(near[1].astype(bf16), "tensor", 1)
    in_grad = join(near[0], first_z, second_z).astype(bf16)

    def weight_grad(left, right):
        return lax.dot_general(left, right, TN, preferred_element_type=f32).astype(bf16)[None]

    return (
        in_grad,
        weight_grad(grad_pre_gate, rows_x),
        weight_grad(grad_pre_up, rows_x),
        weight_grad(hidden, rows_e),
    )


def solution(mesh):
    in_specs = (
        P("expert", "tensor"),
        P("expert", "tensor"),
        P("expert", None),
        P("expert", None),
        P("expert", "tensor", None),
        P("expert", "tensor", None),
        P("expert", "tensor", None),
    )
    out_specs = (
        P("expert", "tensor"),
        P("expert", "tensor", None),
        P("expert", "tensor", None),
        P("expert", "tensor", None),
    )
    groups, tensors = mesh.shape["expert"], mesh.shape["tensor"]
    shards = gather_shards if (groups, tensors) == (8, 4) else dispatch_shards
    return jax.shard_map(shards, mesh=mesh, in_specs=in_specs, out_specs=out_specs, check_vma=False)
```
